32 devices in a mesh: grp: 2 (over y), orient: 4 (over z), rows: 4 (over x, core).
Axes of the slice: x: 2, y: 2, z: 4, core: 2. Of those that a mesh axis runs over, the one named last changes fastest.
Arguments:
- micrograph: bfloat16 [1024, 512], P(('grp', 'rows')), parts along dimension 0, may hold values from -6 to 6
- bank: bfloat16 [20, 512, 512], P(None, 'rows'), may hold values from -0.01171875 to 0.01171875
- orient_index: int32 [16], P('orient'), may hold values from 0 to 19
- noise_power: float32 [1024, 512], P('grp'), parts along dimension 0, may hold values from 0.25 to 4
- defocus: float32 [2], P('grp'), parts along dimension 0, may hold values from 150 to 300
Outputs:
- peak: float32 [1024, 512], P(('grp', 'rows'), 'orient'), parts along dimension 0
- total: float32 [1024, 512], P(('grp', 'rows'), 'orient'), parts along dimension 0
- squares: float32 [1024, 512], P(('grp', 'rows'), 'orient'), parts along dimension 0
The draws below stay inside these ranges and needn't reach their ends.
There are 2 independent parts, one for each index of `grp`. The reference program is written for one: setup_inputs(seed, part) draws one part's arguments, and reference() takes and returns one part's arrays. A program takes and returns all parts, laid end to end along the dimension named above; an argument that names none is the same for every part. Nothing has to cross between parts.
All inputs are finite; a program needn't handle non-finite values.
Results may differ from the reference program's by a relative error of at most 0.0077.
Values may be sent and summed in bfloat16 or wider, within the bound.
A program may use at most 64 MiB of HBM per device.

```python
import math
import jax
import jax.numpy as jnp
from jax import lax

S = 512
MROWS = 512
COLS = 512
ORIENTS = 16
NPROJ = 20


def with_ends(drawn, rng, low, high):
    index_at = [jax.random.randint(jax.random.fold_in(rng, axis), (), 0, length) for axis, length in enumerate(drawn.shape)]
    main_axis = drawn.shape.index(max(drawn.shape))
    beside = index_at[:main_axis] + [(index_at[main_axis] + 1) % drawn.shape[main_axis]] + index_at[main_axis + 1:]
    return drawn.at[tuple(index_at)].set(low).at[tuple(beside)].set(high)


def block_scale(rng, extent, cuts, smallest, high):
    gain, own = 1.0, jax.random.fold_in(rng, 6)
    for dim, blocks in cuts:
        heights = jnp.exp(jax.random.uniform(jax.random.fold_in(own, dim), (blocks,), jnp.float32, smallest / len(cuts), high / len(cuts)))
        gain = gain * jnp.repeat(heights, extent[dim] // blocks).reshape([-1 if axis == dim else 1 for axis in range(len(extent))])
    return gain


def scatter_about(key, extent, deviation, most, cuts=(), dtype=jnp.bfloat16):
    loudness = block_scale(key, extent, cuts, -0.22, 0.18) if cuts else 1.0
    values = jax.random.normal(key, extent, jnp.float32) * deviation * loudness
    return jnp.minimum(jnp.maximum(values, -most), most).astype(dtype)


def setup_inputs(seed: int = 0, part: int = 0) -> dict:
    keys = jax.random.split(jax.random.key(seed), 6)
    part_splits = jax.random.split(jax.random.fold_in(keys[5], part), 6)
    micrograph = scatter_about(part_splits[0], (MROWS, COLS), 1.0, 6.0, ((0, 4),))
    bank = scatter_about(keys[1], (NPROJ, S, S), (S * S) ** -0.5, 0.01171875, ((1, 4),))
    orient_index = with_ends(jax.random.randint(keys[2], (ORIENTS,), 0, NPROJ), jax.random.fold_in(keys[2], 1), 0, NPROJ - 1).astype(jnp.int32)
    noise_power = jnp.clip(jnp.exp(jax.random.uniform(part_splits[3], (MROWS, COLS), jnp.float32, math.log(0.25), math.log(4.0))), 0.25, 4.0)
    defocus = jnp.clip(jax.random.uniform(part_splits[4], (1,), jnp.float32, 150.0, 300.0), 150.0, 300.0)
    return dict(micrograph=micrograph, bank=bank, orient_index=orient_index, noise_power=noise_power, defocus=defocus)


def tables(count, first, nrows, ncols):
    left = lax.iota(jnp.int32, nrows)[:, None] + first
    right = lax.iota(jnp.int32, ncols)[None, :]
    phase = (left * right % count).astype(jnp.float32) * (2.0 * math.pi / count)
    return (jnp.cos(phase).astype(jnp.bfloat16), jnp.sin(phase).astype(jnp.bfloat16))

def spectral_filter(row_ids, col_ids, nrows, ncols, defocus_value, noise):
    freq_y = ((row_ids + nrows // 2) % nrows - nrows // 2).astype(jnp.float32) / nrows
    freq_x = ((col_ids + ncols // 2) % ncols - ncols // 2).astype(jnp.float32) / ncols
    radius = freq_y[:, None] ** 2 + freq_x[None, :] ** 2
    chi = math.pi * defocus_value * radius
    return -(0.9975 * jnp.sin(chi) + 0.07 * jnp.cos(chi)) * lax.rsqrt(noise)

def mm(a, b):
    return jnp.dot(a, b, preferred_element_type=jnp.float32)

def reference(micrograph, bank, orient_index, noise_power, defocus):
    nrows, ncols = micrograph.shape
    side = bank.shape[1]
    lcos, lsin = tables(nrows, 0, nrows, nrows)
    ccos, csin = tables(ncols, 0, ncols, ncols)
    mic_re = mm(micrograph, ccos.T).astype(jnp.bfloat16)
    mic_im = (-mm(micrograph, csin.T)).astype(jnp.bfloat16)
    spec_re = mm(lcos, mic_re) + mm(lsin, mic_im)
    spec_im = mm(lcos, mic_im) - mm(lsin, mic_re)
    filt = spectral_filter(lax.iota(jnp.int32, nrows), lax.iota(jnp.int32, ncols), nrows, ncols, defocus[0], noise_power)
    scale = 1.0 / (nrows * ncols)
    tcos = ccos[:, :side].T
    tsin = csin[:, :side].T
    lcos_t = lcos[:, :side]
    lsin_t = lsin[:, :side]

    def step(carry, index):
        proj = lax.dynamic_index_in_dim(bank, index.astype(jnp.int32), 0, keepdims=False)
        tmp_re = mm(proj, tcos).astype(jnp.bfloat16)
        tmp_im = (-mm(proj, tsin)).astype(jnp.bfloat16)
        proj_re = mm(lcos_t, tmp_re) + mm(lsin_t, tmp_im)
        proj_im = mm(lcos_t, tmp_im) - mm(lsin_t, tmp_re)
        cross_re = (filt * (spec_re * proj_re + spec_im * proj_im)).astype(jnp.bfloat16)
        cross_im = (filt * (spec_im * proj_re - spec_re * proj_im)).astype(jnp.bfloat16)
        half_re = (mm(lcos, cross_re) - mm(lsin, cross_im)).astype(jnp.bfloat16)
        half_im = (mm(lcos, cross_im) + mm(lsin, cross_re)).astype(jnp.bfloat16)
        corr = (mm(half_re, ccos) - mm(half_im, csin)) * scale
        best, summed, squared = carry
        return ((jnp.maximum(best, corr), summed + corr, squared + corr * corr), None)
    start = (jnp.full((nrows, ncols), -jnp.inf, jnp.float32), jnp.zeros((nrows, ncols), jnp.float32), jnp.zeros((nrows, ncols), jnp.float32))
    (peak, total, squares), _ = lax.scan(step, start, orient_index)
    return (peak, total, squares)
```

```python
import functools
import math

import jax
import jax.numpy as jnp
import numpy as np
from jax import lax
from jax.experimental import pallas as pl
from jax.experimental.pallas import tpu as pltpu
from jax.sharding import PartitionSpec as P


def tables(count, nrows, ncols):
    left = lax.iota(jnp.int32, nrows)[:, None]
    right = lax.iota(jnp.int32, ncols)[None, :]
    phase = (left * right % count).astype(jnp.float32) * (2.0 * math.pi / count)
    return (jnp.cos(phase).astype(jnp.bfloat16), jnp.sin(phase).astype(jnp.bfloat16))


def spectral_filter(row_ids, col_ids, nrows, ncols, defocus_value, noise):
    freq_y = ((row_ids + nrows // 2) % nrows - nrows // 2).astype(jnp.float32) / nrows
    freq_x = ((col_ids + ncols // 2) % ncols - ncols // 2).astype(jnp.float32) / ncols
    radius = freq_y[:, None] ** 2 + freq_x[None, :] ** 2
    chi = math.pi * defocus_value * radius
    return -(0.9975 * jnp.sin(chi) + 0.07 * jnp.cos(chi)) * lax.rsqrt(noise)


def mm(a, b):
    return jnp.dot(a, b, preferred_element_type=jnp.float32)


def general(micrograph, bank, orient_index, noise_power, defocus):
    slab, ncols = micrograph.shape
    n_rows = lax.axis_size("rows")
    nrows = slab * n_rows
    row_pos = lax.axis_index("rows")
    lcos, lsin = tables(nrows, nrows, nrows)
    ccos, csin = tables(ncols, ncols, ncols)
    piece = lax.all_gather(micrograph, "rows", axis=0, tiled=True)
    part_re = mm(piece, ccos.T).astype(jnp.bfloat16)
    part_im = (-mm(piece, csin.T)).astype(jnp.bfloat16)
    new_re = mm(lcos, part_re) + mm(lsin, part_im)
    new_im = mm(lcos, part_im) - mm(lsin, part_re)
    chosen = jnp.take(bank, orient_index, axis=0)
    mine = lax.all_to_all(chosen, "rows", split_axis=0, concat_axis=1, tiled=True)
    filt = spectral_filter(
        lax.iota(jnp.int32, nrows),
        lax.iota(jnp.int32, ncols),
        nrows,
        ncols,
        defocus[0],
        noise_power,
    )
    scale = 1.0 / (nrows * ncols)
    tcos = ccos.T
    tsin = csin.T

    def correlate(carry, proj):
        tmp_re = mm(proj, tcos).astype(jnp.bfloat16)
        tmp_im = (-mm(proj, tsin)).astype(jnp.bfloat16)
        proj_re = mm(lcos, tmp_re) + mm(lsin, tmp_im)
        proj_im = mm(lcos, tmp_im) - mm(lsin, tmp_re)
        cross_re = (filt * (new_re * proj_re + new_im * proj_im)).astype(jnp.bfloat16)
        cross_im = (filt * (new_im * proj_re - new_re * proj_im)).astype(jnp.bfloat16)
        half_re = (mm(lcos, cross_re) - mm(lsin, cross_im)).astype(jnp.bfloat16)
        half_im = (mm(lcos, cross_im) + mm(lsin, cross_re)).astype(jnp.bfloat16)
        corr = (mm(half_re, ccos) - mm(half_im, csin)) * scale
        best_now, sum_now, square_now = carry
        return ((jnp.maximum(best_now, corr), sum_now + corr, square_now + corr * corr), None)

    start = (
        jnp.full((nrows, ncols), -jnp.inf, jnp.float32),
        jnp.zeros((nrows, ncols), jnp.float32),
        jnp.zeros((nrows, ncols), jnp.float32),
    )
    (best, summed, squared), _ = lax.scan(correlate, start, mine)
    width = ncols // lax.axis_size("orient")
    best = lax.pmax(best, ("orient", "rows"))
    summed, squared = lax.psum((summed, squared), ("orient", "rows"))
    first_col = lax.axis_index("orient") * width
    first_row = row_pos * slab

    def block(field):
        picked = lax.dynamic_slice_in_dim(field, first_row, slab, 0)
        return lax.dynamic_slice_in_dim(picked, first_col, width, 1)

    peak = block(best)
    total = block(summed)
    squares = block(squared)
    return (peak, total, squares)

MESH = pl.DeviceIdType.MESH


def split_tables(count):
    index = np.arange(count)
    phase = (index[:, None] * index[None, :] % count).astype(np.float32) * np.float32(2.0 * math.pi / count)
    cos = np.cos(phase).astype(jnp.bfloat16).astype(np.float32)
    sin = np.sin(phase).astype(jnp.bfloat16).astype(np.float32)
    mid = count // 2
    wide = np.concatenate([sin, cos, -sin], axis=1)
    forward = np.concatenate([cos[:, :mid + 1], -sin[:, 1:mid]], axis=1)
    backward = np.concatenate([cos[:1], 2 * cos[1:mid], cos[mid:mid + 1], -2 * sin[1:mid]], axis=0) / (count * count)
    mirror = ((index[:, None] + index[None, :]) % count == 0).astype(np.float32)
    across = ((index[:mid, None] + index[None, :mid]) % mid == 0).astype(np.float32)
    return [t.astype(jnp.bfloat16) for t in (wide, forward, backward, mirror, across)]


def dot(a, b):
    return jnp.dot(a, b, preferred_element_type=jnp.float32)


CHUNKS = 2


def kernel(n, m, size, defocus, index, mic_hbm, bank_hbm, noise_hbm, wide_hbm, forward_hbm, backward_hbm, mirror_hbm, across_hbm,
           peak, total, squares,
           bank, chosen, mic, noise, table, forward, backward, mirror, across, mics, remotes, beside, tmp_mic, tmp,
           spec_cos, spec_sin, proj_cos, proj_sin, filt, filt_mid, cross, half,
           far_stage, far_inbox, stage, inbox, part,
           local_sem, near, far_send, far_recv, out_send, out_recv):
    row = lax.axis_index("rows")
    col = lax.axis_index("orient")
    slab = size // n
    width = size // m
    mid = size // 2
    me = row * 2 + lax.rem(col, 2)
    grp = lax.axis_index("grp")
    over = row + 2 - 4 * (row // 2)
    mate = row + 1 - 2 * lax.rem(row, 2)
    corner = mate + 2 - 4 * (mate // 2)
    relay = slab * 3 // 8
    barrier = pltpu.get_barrier_semaphore()
    low = 2 * (col // 2)
    far = 2 - low
    for a in range(n):
        for b in range(2):
            if a or b:
                peer = {"rows": lax.rem(row + a, n), "orient": low + lax.rem(col + b, 2)}
                pl.semaphore_signal(barrier, inc=1, device_id=peer, device_id_type=MESH)
    twin = {"orient": far + lax.rem(col, 2)}
    pl.semaphore_signal(barrier, inc=1, device_id=twin, device_id_type=MESH)
    pl.semaphore_signal(barrier, inc=1, device_id={"grp": 1 - grp}, device_id_type=MESH)
    bank_in = pltpu.make_async_copy(bank_hbm, bank, local_sem.at[0])
    mic_in = pltpu.make_async_copy(mic_hbm, mic, local_sem.at[1])
    forward_in = pltpu.make_async_copy(forward_hbm, forward, local_sem.at[2])
    noise_in = pltpu.make_async_copy(noise_hbm, noise, local_sem.at[3])
    across_in = pltpu.make_async_copy(across_hbm, across, local_sem.at[4])
    mirror_in = pltpu.make_async_copy(mirror_hbm, mirror, local_sem.at[5])
    table_in = pltpu.make_async_copy(wide_hbm, table, local_sem.at[6])
    backward_in = pltpu.make_async_copy(backward_hbm, backward, local_sem.at[7])
    bank_in.start()
    mic_in.start()
    bank_in.wait()
    for copy in (forward_in, noise_in, across_in, mirror_in, table_in, backward_in):
        copy.start()
    for d in (over, corner):
        chosen[d] = bank[index[d]]
    mic_in.wait()
    pl.semaphore_wait(barrier, 2 * n + 1)

    def remote(src, dst, sems, at, to):
        return pltpu.make_async_remote_copy(
            src_ref=src, dst_ref=dst, send_sem=sems.at[0, at], recv_sem=sems.at[1, at],
            device_id=to, device_id_type=MESH)

    passed = pl.ds(grp * (slab - relay), relay)
    kept = pl.ds(relay, slab - 2 * relay)
    bank_over = remote(chosen.at[over, passed], remotes.at[0, passed], near, 0, {"rows": over})
    bank_corner = remote(chosen.at[corner, passed], remotes.at[1, passed], near, 1, {"rows": corner})
    bank_mate = remote(chosen.at[mate], beside.at[0], near, 2, {"rows": mate})
    mic_over = remote(mic, mics.at[0], near, 3, {"rows": over})
    mic_mate = remote(mic, mics.at[1], near, 4, {"rows": mate})
    mic_pass = remote(mics.at[0], mics.at[2], near, 5, {"rows": mate})
    pass_over = remote(remotes.at[0, passed], remotes.at[0, passed], near, 6, {"grp": 1 - grp})
    pass_corner = remote(remotes.at[1, passed], remotes.at[1, passed], near, 7, {"grp": 1 - grp})
    kept_over = remote(chosen.at[over, kept], remotes.at[0, kept], near, 8, {"rows": over})
    kept_corner = remote(chosen.at[corner, kept], remotes.at[1, kept], near, 9, {"rows": corner})
    bank_over.start()
    bank_corner.start()
    mic_over.start()
    mic_mate.start()
    kept_over.start()
    kept_corner.start()
    for d in (mate, row):
        chosen[d] = bank[index[d]]

    def row_dft(into, block, source):
        at = pl.multiple_of(source * slab, slab)
        into[pl.ds(at, slab), :] = dot(block, forward[...]).astype(jnp.bfloat16)

    forward_in.wait()
    row_dft(tmp_mic, mic[...], row)
    bank_mate.start()
    row_dft(tmp, chosen[row], row)
    mic_mate.wait_recv()
    row_dft(tmp_mic, mics[1], mate)
    bank_mate.wait_recv()
    row_dft(tmp, beside[0], mate)
    bank_over.wait_recv()
    pass_over.start()
    noise_in.wait()
    across_in.wait()
    mirror_in.wait()
    noise[...] = lax.rsqrt(noise[...])
    turned = dot(noise[:, mid:].astype(jnp.bfloat16), across[...])
    filt_mid[...] = turned[:, :128]
    flipped = dot(mirror[...], jnp.concatenate([turned.astype(jnp.bfloat16), noise[:, :128].astype(jnp.bfloat16)], axis=1))
    bank_corner.wait_recv()
    pass_corner.start()

    def freq_angle(shape, dim):
        k = lax.broadcasted_iota(jnp.int32, shape, dim)
        f = jnp.where(k < mid, k, k - size).astype(jnp.float32) / size
        return math.pi * defocus[0] * f * f

    angle_x = freq_angle((8, size), 1)
    sin_x = jnp.sin(angle_x)[0:1]
    cos_x = jnp.cos(angle_x)[0:1]
    left_x = -0.5 * (0.9975 * cos_x - 0.07 * sin_x)
    right_x = -0.5 * (0.9975 * sin_x + 0.07 * cos_x)
    down = freq_angle((size, 128), 0)
    sin_y = jnp.sin(down)[:, 0:1]
    cos_y = jnp.cos(down)[:, 0:1]
    edge = lax.broadcasted_iota(jnp.int32, (1, 128), 1) == 0
    both = jnp.concatenate([jnp.where(edge, flipped[:, mid:], flipped[:, :128]), flipped[:, 128:mid]], axis=1)
    filt[...] = (sin_y * left_x[:, :mid] + cos_y * right_x[:, :mid]) * (noise[:, :mid] + both)
    middle = (sin_y * left_x[:, mid:mid + 128] + cos_y * right_x[:, mid:mid + 128]) * (filt_mid[...] + flipped[:, :128])
    filt_mid[...] = jnp.where(edge, middle, 0.0)

    step = 256
    home = (row // 2) * 2 * slab
    away = (1 - row // 2) * 2 * slab
    table_in.wait()

    def rows_at(first):
        return pl.ds(pl.multiple_of(first, 2 * slab), 2 * slab)

    def partial_cos(rows_g, first, source):
        return dot(table[rows_g, rows_at(size + first)], source[rows_at(first), :])

    def partial_sin(rows_g, first, source):
        return dot(table[rows_g, rows_at(first)], source[rows_at(first), :])

    for g in range(size // step):
        rows_g = slice(g * step, (g + 1) * step)
        spec_cos[rows_g, :] = partial_cos(rows_g, home, tmp_mic)
        spec_sin[rows_g, :] = partial_sin(rows_g, home, tmp_mic)
        proj_cos[rows_g, :] = partial_cos(rows_g, home, tmp)
        proj_sin[rows_g, :] = partial_sin(rows_g, home, tmp)
    backward_in.wait()
    mic_over.wait_recv()
    mic_pass.start()
    row_dft(tmp_mic, mics[0], over)
    pass_over.wait_recv()
    kept_over.wait_recv()
    row_dft(tmp, remotes[0], over)
    mic_pass.wait_recv()
    row_dft(tmp_mic, mics[2], corner)
    pass_corner.wait_recv()
    kept_corner.wait_recv()
    row_dft(tmp, remotes[1], corner)
    inner = (lax.broadcasted_iota(jnp.int32, (1, mid), 1) > 0).astype(jnp.float32)
    for g in range(size // step):
        rows_g = slice(g * step, (g + 1) * step)
        s_cos = spec_cos[rows_g, :] + partial_cos(rows_g, away, tmp_mic)
        s_sin = spec_sin[rows_g, :] + partial_sin(rows_g, away, tmp_mic)
        p_cos = proj_cos[rows_g, :] + partial_cos(rows_g, away, tmp)
        p_sin = proj_sin[rows_g, :] + partial_sin(rows_g, away, tmp)
        s_re = s_cos[:, :mid] + inner * s_sin[:, mid:]
        s_im = inner * s_cos[:, mid:] - s_sin[:, :mid]
        p_re = p_cos[:, :mid] + inner * p_sin[:, mid:]
        p_im = inner * p_cos[:, mid:] - p_sin[:, :mid]
        c_re = filt[rows_g, :] * (s_re * p_re + s_im * p_im)
        c_im = filt[rows_g, :] * (s_im * p_re - s_re * p_im)
        lane = slice(mid, mid + 128)
        m_re = filt_mid[rows_g, :] * (s_cos[:, lane] * p_cos[:, lane] + s_sin[:, lane] * p_sin[:, lane])
        m_im = filt_mid[rows_g, :] * (s_cos[:, lane] * p_sin[:, lane] - s_sin[:, lane] * p_cos[:, lane])
        cross[rows_g, :128] = (c_re[:, :128] - m_im).astype(jnp.bfloat16)
        cross[rows_g, 128:] = c_re[:, 128:].astype(jnp.bfloat16)
        rows_i = slice(size + g * step, size + (g + 1) * step)
        cross[rows_i, :128] = (c_im[:, :128] + m_re).astype(jnp.bfloat16)
        cross[rows_i, 128:] = c_im[:, 128:].astype(jnp.bfloat16)

    side = lax.rem(col, 2)
    pairs = n // 2
    short = slab // CHUNKS

    def near_copy(a, b, slot):
        peer = a * 2 + b
        return pltpu.make_async_remote_copy(
            src_ref=stage.at[peer], dst_ref=inbox.at[slot],
            send_sem=out_send.at[peer], recv_sem=out_recv.at[slot],
            device_id={"rows": a, "orient": low + b}, device_id_type=MESH)

    def far_copy(c, a, b, slot):
        peer = a * 2 + b
        return pltpu.make_async_remote_copy(
            src_ref=far_stage.at[c, peer], dst_ref=far_inbox.at[c, slot],
            send_sem=far_send.at[c, peer], recv_sem=far_recv.at[c, slot],
            device_id={"rows": a, "orient": low + b}, device_id_type=MESH)

    def targets(t, s):
        g = lax.rem(row // 2 + t, pairs)
        for i in range(2):
            if t < pairs or i == 0 or s == 1:
                yield g * 2 + lax.rem(row + 1 + i, 2), lax.rem(side + s, 2)

    def corr_of(t, begin):
        at = pl.ds(pl.multiple_of(begin * width, 2 * width), 2 * width)
        return dot(half[t - 1], backward[:, at]).astype(jnp.bfloat16)

    def send_far(t):
        g = lax.rem(row // 2 + t, pairs)
        corr = corr_of(t, far)
        for i in range(2):
            for b in range(2):
                for c in range(CHUNKS):
                    first = i * slab + c * short
                    far_stage[c, (g * 2 + i) * 2 + b] = corr[first:first + short, b * width:(b + 1) * width]
        for c in range(CHUNKS):
            for a, b in (*targets(t, 1), *targets(t, 0)):
                far_copy(c, a, b, me).start()

    def stage_near(t):
        g = lax.rem(row // 2 + t, pairs)
        corr = corr_of(t, low)
        for i in range(2):
            for b in range(2):
                stage[(g * 2 + i) * 2 + b] = corr[i * slab:(i + 1) * slab, b * width:(b + 1) * width]

    def send_near(t, s):
        for a, b in targets(t, s):
            near_copy(a, b, me).start()

    for t in range(1, pairs + 1):
        at = pl.ds(pl.multiple_of(lax.rem(row // 2 + t, pairs) * 2 * slab, 2 * slab), 2 * slab)
        half[t - 1, :, :mid] = dot(table[at, size:], cross[...]).astype(jnp.bfloat16)
        half[t - 1, :, mid:] = dot(table[at, :2 * size], cross[...]).astype(jnp.bfloat16)
        send_far(t)
    for t in range(1, pairs + 1):
        stage_near(t)
    for t in range(1, pairs + 1):
        send_near(t, 0)
    for t in range(1, pairs):
        send_near(t, 1)

    def combine(own, copy_of, box):
        best = summed = own.astype(jnp.float32)
        squared = best * best
        for a in range(n):
            for b in range(2):
                if a or b:
                    ra = lax.rem(row + n - a, n)
                    rb = lax.rem(side + b, 2)
                    source = ra * 2 + rb
                    copy_of(ra, rb, source).wait_recv()
                    value = box[source].astype(jnp.float32)
                    best = jnp.maximum(best, value)
                    summed = summed + value
                    squared = squared + value * value
        return best, summed, squared

    part_copies = []
    for c in range(CHUNKS):
        maps = combine(far_stage[c, me], functools.partial(far_copy, c), far_inbox.at[c])
        for i in range(3):
            part[0, c, i] = maps[i].astype(jnp.bfloat16)
        part_copy = remote(part.at[0, c], part.at[1, c], near, 10 + c, twin)
        part_copy.start()
        part_copies.append(part_copy)
    send_near(pairs, 1)
    best, summed, squared = combine(stage[me], near_copy, inbox)
    for c in range(CHUNKS):
        part_copies[c].wait_recv()
        rows_c = slice(c * short, (c + 1) * short)
        peak[rows_c, :] = jnp.maximum(best[rows_c], part[1, c, 0].astype(jnp.float32))
        total[rows_c, :] = summed[rows_c] + part[1, c, 1].astype(jnp.float32)
        squares[rows_c, :] = squared[rows_c] + part[1, c, 2].astype(jnp.float32)
    for copy in (bank_over, bank_corner, bank_mate, mic_over, mic_mate, mic_pass, pass_over, pass_corner, kept_over, kept_corner, *part_copies):
        copy.wait_send()
    for a in range(n):
        for b in range(2):
            if a or b:
                to = (lax.rem(row + a, n), lax.rem(side + b, 2), me)
                near_copy(*to).wait_send()
                for c in range(CHUNKS):
                    far_copy(c, *to).wait_send()


def write_out(peak_in, total_in, squares_in, peak, total, squares, sems):
    pairs = ((peak_in, peak), (total_in, total), (squares_in, squares))
    writes = [pltpu.make_async_copy(r, w, sems.at[i]) for i, (r, w) in enumerate(pairs)]
    for copy in writes:
        copy.start()
    for copy in writes:
        copy.wait()


def local(micrograph, bank, orient_index, noise_power, defocus):
    slab, size = micrograph.shape
    n = lax.axis_size("rows")
    m = lax.axis_size("orient")
    fits = size == slab * n and n == 4 and m == 4 and lax.axis_size("grp") == 2 and slab % 128 == 0 and (size // m) % 128 == 0 and size & (size - 1) == 0 and size >= 512
    if not (fits and orient_index.shape[0] == n and bank.shape[0] <= 64):
        return general(micrograph, bank, orient_index, noise_power, defocus)
    constants = [jnp.asarray(t) for t in split_tables(size)]
    width = size // m
    mid = size // 2
    out = jax.ShapeDtypeStruct((slab, width), jnp.float32)
    vmem = pl.BlockSpec(memory_space=pltpu.VMEM)
    hbm = pl.BlockSpec(memory_space=pl.ANY)
    smem = pl.BlockSpec(memory_space=pltpu.SMEM)
    bf16 = jnp.bfloat16
    dma = pltpu.SemaphoreType.DMA
    maps = pl.pallas_call(
        functools.partial(kernel, n, m, size),
        out_shape=(out, out, out),
        in_specs=[smem, smem] + [hbm] * 8,
        out_specs=(vmem, vmem, vmem),
        scratch_shapes=[
            pltpu.VMEM(bank.shape, bf16),
            pltpu.VMEM((n, slab, size), bf16),
            pltpu.VMEM((slab, size), bf16),
            pltpu.VMEM((size, size), jnp.float32),
            pltpu.VMEM((size, 3 * size), bf16),
            pltpu.VMEM((size, size), bf16),
            pltpu.VMEM((size, size), bf16),
            pltpu.VMEM((size, size), bf16),
            pltpu.VMEM((mid, mid), bf16),
            pltpu.VMEM((3, slab, size), bf16),
            pltpu.VMEM((2, slab, size), bf16),
            pltpu.VMEM((1, slab, size), bf16),
            pltpu.VMEM((size, size), bf16),
            pltpu.VMEM((size, size), bf16),
            pltpu.VMEM((size, size), jnp.float32),
            pltpu.VMEM((size, size), jnp.float32),
            pltpu.VMEM((size, size), jnp.float32),
            pltpu.VMEM((size, size), jnp.float32),
            pltpu.VMEM((size, mid), jnp.float32),
            pltpu.VMEM((size, 128), jnp.float32),
            pltpu.VMEM((2 * size, mid), bf16),
            pltpu.VMEM((n // 2, 2 * slab, size), bf16),
            pltpu.VMEM((CHUNKS, 2 * n, slab // CHUNKS, width), bf16),
            pltpu.VMEM((CHUNKS, 2 * n, slab // CHUNKS, width), bf16),
            pltpu.VMEM((2 * n, slab, width), bf16),
            pltpu.VMEM((2 * n, slab, width), bf16),
            pltpu.VMEM((2, CHUNKS, 3, slab // CHUNKS, width), bf16),
            dma((8,)), dma((2, 10 + CHUNKS)), dma((CHUNKS, 2 * n)), dma((CHUNKS, 2 * n)), dma((2 * n,)), dma((2 * n,)),
        ],
        compiler_params=pltpu.CompilerParams(collective_id=0, has_side_effects=True, vmem_limit_bytes=55000 * 1024),
        name="correlate",
    )(defocus, orient_index, micrograph, bank, noise_power, *constants)
    return pl.pallas_call(
        write_out,
        out_shape=(out, out, out),
        in_specs=[vmem] * 3,
        out_specs=(hbm, hbm, hbm),
        scratch_shapes=[dma((3,))],
        compiler_params=pltpu.CompilerParams(vmem_limit_bytes=4096 * 1024),
        name="write_out",
    )(*maps)


def solution(mesh):
    in_specs = (
        P(("grp", "rows"), None),
        P(None, "rows", None),
        P("orient"),
        P("grp", None),
        P("grp"),
    )
    out_specs = (
        P(("grp", "rows"), "orient"),
        P(("grp", "rows"), "orient"),
        P(("grp", "rows"), "orient"),
    )
    return jax.shard_map(local, mesh=mesh, in_specs=in_specs, out_specs=out_specs, check_vma=False)
```
